256 devices in a mesh: band: 8 (over z), grid: 32 (over y, x, core).
Axes of the slice: x: 4, y: 4, z: 8, core: 2. Of those that a mesh axis runs over, the one named last changes fastest.
Arguments:
- orbitals: float32 [32, 96, 9216], P('band', 'grid'), may hold values from -6 to 6
- pair_mask: int32 [32, 4], P('band'), may hold values 0 or 1
- cycle_step: int32 [], replicated, may hold values from 1 to 7
Outputs:
- exchange_field: float32 [32, 96, 9216], P('band', 'grid')
- projection: float32 [32, 4], P('band')
The draws below stay inside these ranges and needn't reach their ends.
All inputs are finite; a program needn't handle non-finite values. No bound on the sum of `pair_mask` on one device may be relied on, other than what follows from the above.
Results may differ from the reference program's by a relative error of at most 0.0003.
Values sent between devices are 32-bit elements; how exact they have to be, the bound alone decides.
A program may use at most 64 MiB of HBM per device.

```python
import math
import jax
import jax.numpy as jnp
from jax import lax

B = 4
NX = 96
NY = 96
NZ = 96
ORBS = 32
N_BAND = 8


def with_ends(entries, stream_key, low, high):
    place = [jax.random.randint(jax.random.fold_in(stream_key, axis), (), 0, length) for axis, length in enumerate(entries.shape)]
    longest = entries.shape.index(max(entries.shape))
    beside = place[:longest] + [(place[longest] + 1) % entries.shape[longest]] + place[longest + 1:]
    return entries.at[tuple(place)].set(low).at[tuple(beside)].set(high)


def steps_of(key, extent, pieces, smallest, top_value):
    loudness = 1.0
    for dim, shards_of in pieces:
        steps = jax.random.uniform(jax.random.fold_in(jax.random.fold_in(key, 6), dim), (shards_of,), jnp.float32, smallest / len(pieces), top_value / len(pieces))
        loudness = loudness * jnp.repeat(jnp.exp(steps), extent[dim] // shards_of).reshape((-1,) + (1,) * (len(extent) - 1 - dim))
    return loudness


def normal_values(rng, dims, deviation, limit, pieces=(), kind=jnp.bfloat16):
    gain = steps_of(rng, dims, pieces, -0.22, 0.18) if pieces else 1.0
    drawn = jax.random.normal(rng, dims, jnp.float32) * deviation * gain
    return jnp.minimum(jnp.maximum(drawn, -limit), limit).astype(kind)


def setup_inputs(seed: int = 0) -> dict:
    key_list = jax.random.split(jax.random.key(seed), 4)
    return {
        "orbitals": normal_values(key_list[0], (ORBS, NX, NY * NZ), 1.0, 6.0, ((0, 8), (1, 32)), jnp.float32),
        "pair_mask": with_ends((jax.random.randint(key_list[1], (ORBS, B), 0, 4) < 3).astype(jnp.int32), jax.random.fold_in(key_list[1], 1), 0, 1),
        "cycle_step": jax.random.randint(key_list[2], (), 1, N_BAND).astype(jnp.int32),
    }


box_length = 16.0


def folded(index, length):
    return jnp.where(index * 2 >= length, index - length, index).astype(jnp.float32)


def reference(orbitals, pair_mask, cycle_step):
    orbit_total = orbitals.shape[0]
    fields_full = orbitals.reshape(orbit_total, NX, NY, NZ)
    freq_x = folded(jnp.arange(NX, dtype=jnp.int32), NX)
    freq_y = folded(jnp.arange(NY, dtype=jnp.int32), NY)
    freq_z = folded(jnp.arange(NZ, dtype=jnp.int32), NZ)
    squares = freq_x[:, None, None] ** 2 + freq_y[None, :, None] ** 2 + freq_z[None, None, :] ** 2
    coulomb = box_length * box_length / math.pi
    kernel = jnp.where(squares > 0.5, coulomb / jnp.maximum(squares, 1.0), jnp.float32(0.0))
    mask_float = pair_mask.astype(jnp.float32)

    def one_orbital(index):
        group = index // B
        start = (((group - cycle_step) % N_BAND) * B).astype(jnp.int32)
        visiting = lax.dynamic_slice_in_dim(fields_full, start, B, 0)
        own = lax.dynamic_index_in_dim(fields_full, index, 0, keepdims=False)
        density = own[None] * visiting
        spectra = jnp.fft.fftn(density, axes=(1, 2, 3)) * kernel
        potential = jnp.real(jnp.fft.ifftn(spectra, axes=(1, 2, 3)))
        weights = lax.dynamic_index_in_dim(mask_float, index, 0, keepdims=False)
        return -jnp.einsum('j,jxyz->xyz', weights, potential * visiting, precision=lax.Precision.HIGHEST)

    fields = lax.map(one_orbital, jnp.arange(orbit_total, dtype=jnp.int32))
    exchange_field = fields.reshape(orbit_total, NX, NY * NZ).astype(jnp.float32)
    grouped_orbs = orbitals.reshape(N_BAND, B, NX * NY * NZ)
    grouped_field = exchange_field.reshape(N_BAND, B, NX * NY * NZ)
    projection = jnp.einsum('gar,gcr->gac', grouped_orbs, grouped_field, precision=lax.Precision.HIGHEST)
    projection = (projection / (NX * NY * NZ)).reshape(orbit_total, B)
    return exchange_field, projection
```

```python
import functools
import math

import jax
import jax.numpy as jnp
import numpy as np
from jax import lax
from jax.experimental import pallas as pl
from jax.experimental.pallas import tpu as pltpu
from jax.sharding import PartitionSpec as P

N = 96
LANES = 4 * N
BOX = 16.0
SIDE = 32
EACH = 3
JC = 2
CHUNKS = 4 // JC
ROWS = JC * EACH * EACH * 3
PITCH = -(-ROWS // 8) * 8
MESH = pl.DeviceIdType.MESH


def hartley():
    index = np.arange(N)
    angle = (index[:, None] * index[None, :] % N) * (2.0 * math.pi / N)
    return np.cos(angle) + np.sin(angle)


def two_parts(table):
    high = table.astype(jnp.bfloat16)
    low = (table - high.astype(np.float64)).astype(jnp.bfloat16)
    return high, low


def stacked(table):
    high, low = two_parts(table)
    return np.concatenate([np.concatenate([high, high], 1), np.concatenate([low, low], 1)], 0)


def tables():
    cas = hartley()
    order = np.array([EACH * (r % SIDE) + r // SIDE for r in range(N)])
    out_of = stacked(cas[order, :])
    into = stacked(cas[:, order])
    z_high, z_low = two_parts(np.kron(np.eye(4), cas))
    freq = np.arange(N)
    freq = np.where(freq * 2 >= N, freq - N, freq).astype(np.float32)
    squares = freq[:, None] ** 2 + np.tile(freq, 4)[None, :] ** 2
    pick = np.zeros((LANES, 128), np.float32)
    pick[np.arange(LANES), np.arange(LANES) // N] = 1.0
    return out_of, into, z_high, z_low, squares.astype(np.float32), pick.astype(jnp.bfloat16)


def split(value):
    high = value.astype(jnp.bfloat16)
    low = (value - high.astype(jnp.float32)).astype(jnp.bfloat16)
    return high, low


def dot(a, b):
    return jnp.dot(a, b, preferred_element_type=jnp.float32)


def left(table, value):
    high, low = split(value)
    both = dot(table, jnp.concatenate([high, low], 0))
    return both[:N] + both[N:]


def right(value, z_high, z_low):
    high, low = split(value)
    rows = value.shape[0]
    both = dot(jnp.concatenate([high, low], 0), z_high)
    return both[:rows] + both[rows:] + dot(high, z_low)


def one_orbital(tiles, j):
    a, b, c = tiles
    lane = lax.broadcasted_iota(jnp.int32, a.shape, 1)
    roll = lambda v, s: pltpu.roll(v, s, 1)
    if j == 0:
        v = a
    elif j == 1:
        v = jnp.where(lane < 32, roll(a, 32), roll(b, 32))
    elif j == 2:
        v = jnp.where(lane < 64, roll(b, 64), roll(c, 64))
    else:
        v = roll(c, 96)
    v32, v64, v96 = roll(v, 32), roll(v, 64), roll(v, 96)
    return [
        jnp.where(lane < 96, v, v96),
        jnp.where(lane < 64, v96, v64),
        jnp.where(lane < 32, v64, v32),
    ]


def lane_tiles(value):
    return [value[:, 128 * t : 128 * t + 128] for t in range(3)]


def body(
    own_ref, vis_ref, mask_ref, out_of_ref, into_ref, zh_ref, zl_ref, sq_ref, pick_ref,
    field_ref, proj_ref,
    rep, coulomb, send1, recv1, send2, recv2, part_send, part_recv,
    send_sem, recv_sem, own_sem, part_sems,
):
    me = lax.axis_index("grid")
    barrier = pltpu.get_barrier_semaphore()

    def greet(t, _):
        pl.semaphore_signal(barrier, inc=1, device_id={"grid": (me + t) % SIDE}, device_id_type=MESH)
        return 0

    lax.fori_loop(1, SIDE, greet, 0)

    def densities(c):
        for jj in range(JC):
            j = c * JC + jj

            def plane_step(p, _):
                vis = jnp.concatenate(one_orbital(lane_tiles(vis_ref[p]), j), 1)
                rep[j, p] = vis
                value = right(own_ref[p] * vis, zh_ref[...], zl_ref[...])
                value = left(out_of_ref[...], value)
                for k in range(EACH):
                    for b in range(3):
                        row = ((jj * EACH + p) * EACH + k) * 3 + b
                        send1[c, pl.ds(row, SIDE, stride=PITCH), :] = value[
                            k * SIDE : (k + 1) * SIDE, b * 128 : (b + 1) * 128
                        ]
                return 0

            lax.fori_loop(0, EACH, plane_step, 0)

    def exchange(way, c, send, recv):
        def one(t, _):
            to = (me + t) % SIDE
            pltpu.make_async_remote_copy(
                src_ref=send.at[c, pl.ds(pl.multiple_of(to * PITCH, 8), PITCH)],
                dst_ref=recv.at[c, pl.ds(pl.multiple_of(me * PITCH, 8), PITCH)],
                send_sem=send_sem.at[way, c],
                recv_sem=recv_sem.at[way, c],
                device_id={"grid": to},
                device_id_type=MESH,
            ).start()
            return 0

        lax.fori_loop(1, SIDE, one, 0)
        mine = pl.ds(pl.multiple_of(me * PITCH, 8), PITCH)
        pltpu.make_async_copy(send.at[c, mine], recv.at[c, mine], own_sem.at[way, c]).start()

    def arrived(way, c, send, recv):
        mine = pl.ds(pl.multiple_of(me * PITCH, 8), PITCH)
        pltpu.make_async_copy(send.at[c, mine], recv.at[c, mine], own_sem.at[way, c]).wait()
        most = pl.ds(0, (SIDE - 1) * PITCH)
        pltpu.make_async_copy(recv.at[c, most], recv.at[c, most], recv_sem.at[way, c]).wait()

    def sent(way, c, send):
        most = pl.ds(0, (SIDE - 1) * PITCH)
        pltpu.make_async_copy(send.at[c, most], send.at[c, most], send_sem.at[way, c]).wait()

    def along_x(c):
        for jj in range(JC):

            def row_step(k, _):
                def row(p, b):
                    return ((jj * EACH + p) * EACH + k) * 3 + b

                value = jnp.concatenate(
                    [
                        jnp.concatenate(
                            [recv1[c, pl.ds(row(p, b), SIDE, stride=PITCH), :] for b in range(3)], 1
                        )
                        for p in range(EACH)
                    ],
                    0,
                )
                value = left(into_ref[...], value) * coulomb[k]
                value = left(out_of_ref[...], value)
                for p in range(EACH):
                    for b in range(3):
                        send2[c, pl.ds(row(p, b), SIDE, stride=PITCH), :] = value[
                            p * SIDE : (p + 1) * SIDE, b * 128 : (b + 1) * 128
                        ]
                return 0

            lax.fori_loop(0, EACH, row_step, 0)

    def fields(c):
        for jj in range(JC):
            j = c * JC + jj

            def plane_step(p, _):
                value = jnp.concatenate(
                    [
                        jnp.concatenate(
                            [
                                recv2[
                                    c,
                                    pl.ds(((jj * EACH + p) * EACH + k) * 3 + b, SIDE, stride=PITCH),
                                    :,
                                ]
                                for b in range(3)
                            ],
                            1,
                        )
                        for k in range(EACH)
                    ],
                    0,
                )
                value = left(into_ref[...], value)
                value = right(value, zh_ref[...], zl_ref[...])
                term = value * rep[j, p] * mask_ref[pl.ds(j, 1), :]
                if j == 0:
                    field_ref[p] = -term
                else:
                    field_ref[p] = field_ref[p] - term
                return 0

            lax.fori_loop(0, EACH, plane_step, 0)

    coul = BOX * BOX / math.pi / (N * N * N)
    for k in range(EACH):
        ky = me * EACH + k
        folded = jnp.where(ky * 2 >= N, ky - N, ky).astype(jnp.float32)
        squares = sq_ref[...] + folded * folded
        coulomb[k] = jnp.where(squares > 0.5, coul / jnp.maximum(squares, 1.0), 0.0)

    densities(0)
    pl.semaphore_wait(barrier, SIDE - 1)
    exchange(0, 0, send1, recv1)
    for c in range(1, CHUNKS):
        densities(c)
        exchange(0, c, send1, recv1)
    for c in range(CHUNKS):
        arrived(0, c, send1, recv1)
        along_x(c)
        exchange(1, c, send2, recv2)
    for c in range(CHUNKS):
        arrived(1, c, send2, recv2)
        fields(c)

    rows = []
    for a in range(4):

        def plane_sum(p, total):
            own = jnp.concatenate(one_orbital(lane_tiles(own_ref[p]), a), 1)
            return total + jnp.sum(own * field_ref[p], axis=0, keepdims=True)

        rows.append(lax.fori_loop(0, EACH, plane_sum, jnp.zeros((1, LANES), jnp.float32)))
    sums = jnp.concatenate(rows + [jnp.zeros((4, LANES), jnp.float32)], 0)
    high = sums.astype(jnp.bfloat16)
    rest = sums - high.astype(jnp.float32)
    middle, low = split(rest)
    pick = pick_ref[...]
    sums = dot(high, pick) + dot(middle, pick) + dot(low, pick)
    part_send[...] = sums
    part_recv[me] = sums

    def tell(t, _):
        pltpu.make_async_remote_copy(
            src_ref=part_send,
            dst_ref=part_recv.at[me],
            send_sem=part_sems.at[0],
            recv_sem=part_sems.at[1],
            device_id={"grid": (me + t) % SIDE},
            device_id_type=MESH,
        ).start()
        return 0

    lax.fori_loop(1, SIDE, tell, 0)
    for c in range(CHUNKS):
        sent(0, c, send1)
        sent(1, c, send2)
    most = part_recv.at[pl.ds(0, SIDE - 1)]
    pltpu.make_async_copy(most, most, part_sems.at[1]).wait()
    pltpu.make_async_copy(most, most, part_sems.at[0]).wait()
    proj_ref[...] = jnp.sum(part_recv[...], axis=0) * (1.0 / (N * N * N))


def vmem(count):
    return [pl.BlockSpec(memory_space=pltpu.VMEM)] * count


def shards(orbitals, pair_mask, cycle_step):
    own = orbitals.reshape(4, EACH, N, N).transpose(1, 2, 0, 3).reshape(EACH, N, LANES)

    def moved(distance, block):
        count = lax.axis_size("band")
        return lax.ppermute(block, "band", [((i - distance) % count, i) for i in range(count)])

    visiting = lax.switch(
        cycle_step - 1, [functools.partial(moved, d) for d in range(1, 8)], own
    )
    mask = jnp.repeat(pair_mask.astype(jnp.float32).T, N, axis=1)
    buffer = pltpu.VMEM((CHUNKS, SIDE * PITCH, 128), jnp.float32)
    field, projection = pl.pallas_call(
        body,
        out_shape=(
            jax.ShapeDtypeStruct((EACH, N, LANES), jnp.float32),
            jax.ShapeDtypeStruct((8, 128), jnp.float32),
        ),
        in_specs=vmem(9),
        out_specs=tuple(vmem(2)),
        scratch_shapes=[
            pltpu.VMEM((4, EACH, N, LANES), jnp.float32),
            pltpu.VMEM((EACH, N, LANES), jnp.float32),
            buffer, buffer, buffer, buffer,
            pltpu.VMEM((8, 128), jnp.float32),
            pltpu.VMEM((SIDE, 8, 128), jnp.float32),
            pltpu.SemaphoreType.DMA((2, CHUNKS)),
            pltpu.SemaphoreType.DMA((2, CHUNKS)),
            pltpu.SemaphoreType.DMA((2, CHUNKS)),
            pltpu.SemaphoreType.DMA((2,)),
        ],
        compiler_params=pltpu.CompilerParams(
            collective_id=0, has_side_effects=True, vmem_limit_bytes=40 * 1024 * 1024
        ),
    )(own, visiting, mask, *[jnp.asarray(t) for t in tables()])
    exchange_field = field.reshape(EACH, N, 4, N).transpose(2, 0, 1, 3).reshape(4, EACH, N * N)
    return exchange_field, projection[:4, :4]


def solution(mesh):
    return jax.shard_map(
        shards,
        mesh=mesh,
        in_specs=(P("band", "grid", None), P("band", None), P()),
        out_specs=(P("band", "grid", None), P("band", None)),
        check_vma=False,
    )
```

```python
import functools
import math

import jax
import jax.numpy as jnp
import numpy as np
from jax import lax
from jax.experimental import pallas as pl
from jax.experimental.pallas import tpu as pltpu
from jax.sharding import PartitionSpec as P

N = 96
LANES = 4 * N
BOX = 16.0
SIDE = 32
EACH = 3
CHUNKS = 4
ROWS = EACH * EACH * 3
PITCH = -(-ROWS // 8) * 8
PLANE = N * N // 128
FLAT = EACH * PLANE
BANDS = 8
MESH = pl.DeviceIdType.MESH


def hartley():
    index = np.arange(N)
    angle = (index[:, None] * index[None, :] % N) * (2.0 * math.pi / N)
    return np.cos(angle) + np.sin(angle)


def two_parts(table):
    high = table.astype(jnp.bfloat16)
    low = (table - high.astype(np.float64)).astype(jnp.bfloat16)
    return high, low


def stacked(table):
    high, low = two_parts(table)
    return np.concatenate([np.concatenate([high, high], 1), np.concatenate([low, low], 1)], 0)


def tables():
    cas = hartley()
    order = np.array([EACH * (r % SIDE) + r // SIDE for r in range(N)])
    lines = np.array([4 * (r % 24) + r // 24 for r in range(N)])
    y_out = stacked(cas[order][:, lines])
    y_into = stacked(cas[lines][:, order])
    x_into = stacked(cas[:, order])
    x_out = stacked(cas[order])
    z_high, z_low = two_parts(np.kron(np.eye(4), cas))
    freq = np.arange(N)
    freq = np.where(freq * 2 >= N, freq - N, freq).astype(np.float32)
    squares = freq[:, None] ** 2 + np.tile(freq, 4)[None, :] ** 2
    pick = np.zeros((LANES, 128), np.float32)
    pick[np.arange(LANES), np.arange(LANES) // N] = 1.0
    pick = pick.astype(jnp.bfloat16)
    return y_out, y_into, x_into, x_out, z_high, z_low, squares.astype(np.float32), pick


def split(value):
    high = value.astype(jnp.bfloat16)
    low = (value - high.astype(jnp.float32)).astype(jnp.bfloat16)
    return high, low


def dot(a, b):
    return jnp.dot(a, b, preferred_element_type=jnp.float32)


def left(table, value):
    high, low = split(value)
    both = dot(table, jnp.concatenate([high, low], 0))
    return both[:N] + both[N:]


def right(value, z_high, z_low):
    high, low = split(value)
    rows = value.shape[0]
    both = dot(jnp.concatenate([high, low], 0), z_high)
    return both[:rows] + both[rows:] + dot(high, z_low)


def roll(value, shift):
    return pltpu.roll(value, shift, 1)


def lane_of(value):
    return lax.broadcasted_iota(jnp.int32, value.shape, 1)


def taken(tiles, j):
    a, b, c = tiles
    lane = lane_of(a)
    if j == 0:
        return a
    if j == 1:
        return jnp.where(lane < 32, roll(a, 32), roll(b, 32))
    if j == 2:
        return jnp.where(lane < 64, roll(b, 64), roll(c, 64))
    return roll(c, 96)


def joined(four):
    lane = lane_of(four[0])
    one, two = roll(four[1], 96), roll(four[2], 64)
    return [
        jnp.where(lane < 96, four[0], one),
        jnp.where(lane < 64, one, two),
        jnp.where(lane < 32, two, roll(four[3], 32)),
    ]


def rows_of(ref, j, p):
    return [ref[j, pl.ds(p * PLANE + t, 24, stride=3), :] for t in range(3)]


def repeated(ref, j, p):
    tiles = rows_of(ref, j, p)
    lines = []
    for u in range(4):
        v = taken(tiles, u)
        lines.append(jnp.concatenate(joined([v, v, v, v]), 1))
    return jnp.concatenate(lines, 0)


def side_by_side(ref, p):
    tiles = [rows_of(ref, i, p) for i in range(4)]
    lines = []
    for u in range(4):
        lines.append(jnp.concatenate(joined([taken(tiles[i], u) for i in range(4)]), 1))
    return jnp.concatenate(lines, 0)


def body(
    distance,
    mask_ref, orb_ref, y_out_ref, y_into_ref, x_into_ref, x_out_ref, zh_ref, zl_ref, sq_ref, pick_ref,
    field_ref, proj_ref,
    vis, own, own_rep, rep, field, coulomb, send1, recv1, send2, recv2, part_send, part_recv,
    vis_sems, send_sem, recv_sem, own_sem, part_sems,
):
    me = lax.axis_index("grid")
    band = lax.axis_index("band")
    barrier = pltpu.get_barrier_semaphore()

    def greet(t, _):
        pl.semaphore_signal(barrier, inc=1, device_id={"grid": (me + t) % SIDE}, device_id_type=MESH)
        return 0

    source = (band + BANDS - distance) % BANDS
    pl.semaphore_signal(barrier, inc=1, device_id={"band": source}, device_id_type=MESH)
    lax.fori_loop(1, SIDE, greet, 0)
    pl.semaphore_wait(barrier, SIDE)

    def passing(j):
        return pltpu.make_async_remote_copy(
            src_ref=orb_ref.at[j],
            dst_ref=vis.at[j],
            send_sem=vis_sems.at[0, j],
            recv_sem=vis_sems.at[1, j],
            device_id={"band": (band + distance) % BANDS},
            device_id_type=MESH,
        )

    def chunk_row(p, k, b):
        return (p * EACH + k) * 3 + b

    def densities(c):
        def plane_step(p, _):
            visiting = repeated(vis, c, p)
            rep[c, p] = visiting
            value = right(own[p] * visiting, zh_ref[...], zl_ref[...])
            value = left(y_out_ref[...], value)
            for k in range(EACH):
                for b in range(3):
                    send1[c, pl.ds(chunk_row(p, k, b), SIDE, stride=PITCH), :] = value[
                        k * SIDE : (k + 1) * SIDE, b * 128 : (b + 1) * 128
                    ]
            return 0

        lax.fori_loop(0, EACH, plane_step, 0)

    def to_rows(device):
        return pl.ds(pl.multiple_of(device * PITCH, 8), ROWS)

    def exchange(way, c, send, recv):
        def one(t, _):
            to = (me + t) % SIDE
            pltpu.make_async_remote_copy(
                src_ref=send.at[c, to_rows(to)],
                dst_ref=recv.at[c, to_rows(me)],
                send_sem=send_sem.at[way, c],
                recv_sem=recv_sem.at[way, c],
                device_id={"grid": to},
                device_id_type=MESH,
            ).start()
            return 0

        lax.fori_loop(1, SIDE, one, 0)
        pltpu.make_async_copy(
            send.at[c, to_rows(me)], recv.at[c, to_rows(me)], own_sem.at[way, c]
        ).start()

    most = pl.ds(0, (SIDE - 1) * ROWS)

    def arrived(way, c, send, recv):
        pltpu.make_async_copy(
            send.at[c, to_rows(me)], recv.at[c, to_rows(me)], own_sem.at[way, c]
        ).wait()
        pltpu.make_async_copy(recv.at[c, most], recv.at[c, most], recv_sem.at[way, c]).wait()

    def sent(way, c, send):
        pltpu.make_async_copy(send.at[c, most], send.at[c, most], send_sem.at[way, c]).wait()

    def gathered(recv, c, row):
        return jnp.concatenate(
            [
                jnp.concatenate(
                    [recv[c, pl.ds(row(part, b), SIDE, stride=PITCH), :] for b in range(3)], 1
                )
                for part in range(EACH)
            ],
            0,
        )

    def along_x(c):
        def row_step(k, _):
            value = gathered(recv1, c, lambda p, b: chunk_row(p, k, b))
            value = left(x_into_ref[...], value) * coulomb[k]
            value = left(x_out_ref[...], value)
            for p in range(EACH):
                for b in range(3):
                    send2[c, pl.ds(chunk_row(p, k, b), SIDE, stride=PITCH), :] = value[
                        p * SIDE : (p + 1) * SIDE, b * 128 : (b + 1) * 128
                    ]
            return 0

        lax.fori_loop(0, EACH, row_step, 0)

    lane = lax.broadcasted_iota(jnp.int32, (1, LANES), 1)

    def fields(c):
        weights = [mask_ref[i, c].astype(jnp.float32) for i in range(4)]
        weight = jnp.where(
            lane < 2 * N,
            jnp.where(lane < N, weights[0], weights[1]),
            jnp.where(lane < 3 * N, weights[2], weights[3]),
        )

        def plane_step(p, _):
            value = gathered(recv2, c, lambda k, b: chunk_row(p, k, b))
            value = left(y_into_ref[...], value)
            value = right(value, zh_ref[...], zl_ref[...])
            term = value * rep[c, p] * weight
            if c == 0:
                field[p] = -term
            else:
                field[p] = field[p] - term
            return 0

        lax.fori_loop(0, EACH, plane_step, 0)

    passing(0).start()

    def prepare(p, _):
        own[p] = side_by_side(orb_ref, p)
        for a in range(4):
            own_rep[a, p] = repeated(orb_ref, a, p)
        return 0

    lax.fori_loop(0, EACH, prepare, 0)
    coul = BOX * BOX / math.pi / (N * N * N)
    for k in range(EACH):
        ky = me * EACH + k
        folded = jnp.where(ky * 2 >= N, ky - N, ky).astype(jnp.float32)
        squares = sq_ref[...] + folded * folded
        coulomb[k] = jnp.where(squares > 0.5, coul / jnp.maximum(squares, 1.0), 0.0)

    for c in range(CHUNKS):
        passing(c).wait_recv()
        if c + 1 < CHUNKS:
            passing(c + 1).start()
        densities(c)
        exchange(0, c, send1, recv1)
        if c > 0:
            arrived(0, c - 1, send1, recv1)
            along_x(c - 1)
            exchange(1, c - 1, send2, recv2)
    last = CHUNKS - 1
    arrived(0, last, send1, recv1)
    along_x(last)
    exchange(1, last, send2, recv2)
    for c in range(CHUNKS):
        arrived(1, c, send2, recv2)
        fields(c)

    rows = []
    for a in range(4):

        def plane_sum(p, total):
            return total + jnp.sum(own_rep[a, p] * field[p], axis=0, keepdims=True)

        rows.append(lax.fori_loop(0, EACH, plane_sum, jnp.zeros((1, LANES), jnp.float32)))
    sums = jnp.concatenate(rows + [jnp.zeros((4, LANES), jnp.float32)], 0)
    high = sums.astype(jnp.bfloat16)
    middle, low = split(sums - high.astype(jnp.float32))
    pick = pick_ref[...]
    sums = dot(high, pick) + dot(middle, pick) + dot(low, pick)
    part_send[...] = sums
    part_recv[me] = sums

    def tell(t, _):
        pltpu.make_async_remote_copy(
            src_ref=part_send,
            dst_ref=part_recv.at[me],
            send_sem=part_sems.at[0],
            recv_sem=part_sems.at[1],
            device_id={"grid": (me + t) % SIDE},
            device_id_type=MESH,
        ).start()
        return 0

    lax.fori_loop(1, SIDE, tell, 0)

    def lay_out(p, _):
        tiles = [
            [field[p, 24 * u : 24 * u + 24, 128 * t : 128 * t + 128] for t in range(3)]
            for u in range(4)
        ]
        for i in range(4):
            rows = joined([taken(tiles[u], i) for u in range(4)])
            for t in range(3):
                field_ref[i, pl.ds(p * PLANE + t, 24, stride=3), :] = rows[t]
        return 0

    lax.fori_loop(0, EACH, lay_out, 0)
    for c in range(CHUNKS):
        passing(c).wait_send()
        sent(0, c, send1)
        sent(1, c, send2)
    others = part_recv.at[pl.ds(0, SIDE - 1)]
    pltpu.make_async_copy(others, others, part_sems.at[1]).wait()
    pltpu.make_async_copy(others, others, part_sems.at[0]).wait()
    proj_ref[...] = jnp.sum(part_recv[...], axis=0) * (1.0 / (N * N * N))


def vmem(count):
    return [pl.BlockSpec(memory_space=pltpu.VMEM)] * count


def at_distance(distance, mask, orbitals, *constants):
    def scratch(*shape):
        return pltpu.VMEM(shape, jnp.float32)

    buffer = scratch(CHUNKS, SIDE * PITCH, 128)
    return pl.pallas_call(
        functools.partial(body, distance),
        out_shape=(
            jax.ShapeDtypeStruct((4, FLAT, 128), jnp.float32),
            jax.ShapeDtypeStruct((8, 128), jnp.float32),
        ),
        in_specs=[pl.BlockSpec(memory_space=pltpu.SMEM)] + vmem(1 + len(constants)),
        out_specs=tuple(vmem(2)),
        scratch_shapes=[
            scratch(4, FLAT, 128),
            scratch(EACH, N, LANES),
            scratch(4, EACH, N, LANES),
            scratch(4, EACH, N, LANES),
            scratch(EACH, N, LANES),
            scratch(EACH, N, LANES),
            buffer, buffer, buffer, buffer,
            scratch(8, 128),
            scratch(SIDE, 8, 128),
            pltpu.SemaphoreType.DMA((2, CHUNKS)),
            pltpu.SemaphoreType.DMA((2, CHUNKS)),
            pltpu.SemaphoreType.DMA((2, CHUNKS)),
            pltpu.SemaphoreType.DMA((2, CHUNKS)),
            pltpu.SemaphoreType.DMA((2,)),
        ],
        compiler_params=pltpu.CompilerParams(
            collective_id=distance - 1, has_side_effects=True, vmem_limit_bytes=40 * 1024 * 1024
        ),
        name=f"exchange_{distance}",
    )(mask, orbitals, *constants)


def shards(orbitals, pair_mask, cycle_step):
    constants = [jnp.asarray(t) for t in tables()]
    field, projection = lax.switch(
        cycle_step - 1,
        [functools.partial(at_distance, d) for d in range(1, BANDS)],
        pair_mask,
        orbitals.reshape(4, FLAT, 128),
        *constants,
    )
    return field.reshape(4, EACH, N * N), projection[:4, :4]


def solution(mesh):
    return jax.shard_map(
        shards,
        mesh=mesh,
        in_specs=(P("band", "grid", None), P("band", None), P()),
        out_specs=(P("band", "grid", None), P("band", None)),
        check_vma=False,
    )
```

```python
import functools
import math

import jax
import jax.numpy as jnp
import numpy as np
from jax import lax
from jax.experimental import pallas as pl
from jax.experimental.pallas import tpu as pltpu
from jax.sharding import PartitionSpec as P

N = 96
LANES = 4 * N
BOX = 16.0
SIDE = 32
EACH = 3
CHUNKS = 4
ROWS = EACH * EACH * 3
PITCH = -(-ROWS // 8) * 8
PLANE = N * N // 128
FLAT = EACH * PLANE
BANDS = 8
MESH = pl.DeviceIdType.MESH


def hartley():
    index = np.arange(N)
    angle = (index[:, None] * index[None, :] % N) * (2.0 * math.pi / N)
    return np.cos(angle) + np.sin(angle)


def two_parts(table):
    high = table.astype(jnp.bfloat16)
    low = (table - high.astype(np.float64)).astype(jnp.bfloat16)
    return high, low


def stacked(table):
    high, low = two_parts(table)
    return np.concatenate([np.concatenate([high, high], 1), np.concatenate([low, low], 1)], 0)


def tables():
    cas = hartley()
    order = np.array([EACH * (r % SIDE) + r // SIDE for r in range(N)])
    lines = np.array([4 * (r % 24) + r // 24 for r in range(N)])
    y_out = stacked(cas[order][:, lines])
    y_into = stacked(cas[lines][:, order])
    x_into = stacked(cas[:, order])
    x_out = stacked(cas[order])
    z_high, z_low = two_parts(np.kron(np.eye(4), cas))
    freq = np.arange(N)
    freq = np.where(freq * 2 >= N, freq - N, freq).astype(np.float32)
    squares = freq[:, None] ** 2 + np.tile(freq, 4)[None, :] ** 2
    pick = np.zeros((LANES, 128), np.float32)
    pick[np.arange(LANES), np.arange(LANES) // N] = 1.0
    pick = pick.astype(jnp.bfloat16)
    return y_out, y_into, x_into, x_out, z_high, z_low, squares.astype(np.float32), pick


def split(value):
    high = value.astype(jnp.bfloat16)
    low = (value - high.astype(jnp.float32)).astype(jnp.bfloat16)
    return high, low


def dot(a, b):
    return jnp.dot(a, b, preferred_element_type=jnp.float32)


def left(table, value):
    high, low = split(value)
    both = dot(table, jnp.concatenate([high, low], 0))
    return both[:N] + both[N:]


def right(value, z_high, z_low):
    high, low = split(value)
    rows = value.shape[0]
    both = dot(jnp.concatenate([high, low], 0), z_high)
    return both[:rows] + both[rows:] + dot(high, z_low)


def roll(value, shift):
    return pltpu.roll(value, shift, 1)


def lane_of(value):
    return lax.broadcasted_iota(jnp.int32, value.shape, 1)


def taken(tiles, j):
    a, b, c = tiles
    lane = lane_of(a)
    if j == 0:
        return a
    if j == 1:
        return jnp.where(lane < 32, roll(a, 32), roll(b, 32))
    if j == 2:
        return jnp.where(lane < 64, roll(b, 64), roll(c, 64))
    return roll(c, 96)


def joined(four):
    lane = lane_of(four[0])
    one, two = roll(four[1], 96), roll(four[2], 64)
    return [
        jnp.where(lane < 96, four[0], one),
        jnp.where(lane < 64, one, two),
        jnp.where(lane < 32, two, roll(four[3], 32)),
    ]


def turned(value, d):
    if d == 0:
        return value
    tiles = lane_tiles(value)
    rolled = [roll(t, 32 * d) for t in tiles]
    lane = lane_of(tiles[0])
    first = {1: 0, 2: 1, 3: 2}[d]
    return jnp.concatenate(
        [
            jnp.where(lane < 32 * d, rolled[(t + first) % 3], rolled[(t + first + 1) % 3])
            for t in range(3)
        ],
        1,
    )


def lane_tiles(value):
    return [value[:, 128 * t : 128 * t + 128] for t in range(3)]


def rows_of(ref, j, p):
    return [ref[j, pl.ds(p * PLANE + t, 24, stride=3), :] for t in range(3)]


def repeated(ref, j, p):
    tiles = rows_of(ref, j, p)
    lines = []
    for u in range(4):
        v = taken(tiles, u)
        lines.append(jnp.concatenate(joined([v, v, v, v]), 1))
    return jnp.concatenate(lines, 0)


def side_by_side(ref, p):
    tiles = [rows_of(ref, i, p) for i in range(4)]
    lines = []
    for u in range(4):
        lines.append(jnp.concatenate(joined([taken(tiles[i], u) for i in range(4)]), 1))
    return jnp.concatenate(lines, 0)


def body(
    distance,
    mask_ref, orb_ref, y_out_ref, y_into_ref, x_into_ref, x_out_ref, zh_ref, zl_ref, sq_ref, pick_ref,
    field_ref, proj_ref,
    vis, own, gram, rep, field, coulomb, send1, recv1, send2, recv2, part_send, part_recv,
    vis_sems, send_sem, recv_sem, own_sem, part_sems,
):
    me = lax.axis_index("grid")
    band = lax.axis_index("band")
    barrier = pltpu.get_barrier_semaphore()

    def greet(t, _):
        pl.semaphore_signal(barrier, inc=1, device_id={"grid": (me + t) % SIDE}, device_id_type=MESH)
        return 0

    source = (band + BANDS - distance) % BANDS
    pl.semaphore_signal(barrier, inc=1, device_id={"band": source}, device_id_type=MESH)
    lax.fori_loop(1, SIDE, greet, 0)

    def passing(j):
        return pltpu.make_async_remote_copy(
            src_ref=orb_ref.at[j],
            dst_ref=vis.at[j],
            send_sem=vis_sems.at[0, j],
            recv_sem=vis_sems.at[1, j],
            device_id={"band": (band + distance) % BANDS},
            device_id_type=MESH,
        )

    def chunk_row(p, k, b):
        return (p * EACH + k) * 3 + b

    def densities(c):
        def plane_step(p, _):
            visiting = repeated(vis, c, p)
            rep[c, p] = visiting
            value = right(own[p] * visiting, zh_ref[...], zl_ref[...])
            value = left(y_out_ref[...], value)
            for k in range(EACH):
                for b in range(3):
                    send1[c, pl.ds(chunk_row(p, k, b), SIDE, stride=PITCH), :] = value[
                        k * SIDE : (k + 1) * SIDE, b * 128 : (b + 1) * 128
                    ]
            return 0

        lax.fori_loop(0, EACH, plane_step, 0)

    def to_rows(device):
        return pl.ds(pl.multiple_of(device * PITCH, 8), ROWS)

    def exchange(way, c, send, recv):
        def one(t, _):
            to = (me + t) % SIDE
            pltpu.make_async_remote_copy(
                src_ref=send.at[c, to_rows(to)],
                dst_ref=recv.at[c, to_rows(me)],
                send_sem=send_sem.at[way, c],
                recv_sem=recv_sem.at[way, c],
                device_id={"grid": to},
                device_id_type=MESH,
            ).start()
            return 0

        lax.fori_loop(1, SIDE, one, 0)
        pltpu.make_async_copy(
            send.at[c, to_rows(me)], recv.at[c, to_rows(me)], own_sem.at[way, c]
        ).start()

    most = pl.ds(0, (SIDE - 1) * ROWS)

    def arrived(way, c, send, recv):
        pltpu.make_async_copy(
            send.at[c, to_rows(me)], recv.at[c, to_rows(me)], own_sem.at[way, c]
        ).wait()
        pltpu.make_async_copy(recv.at[c, most], recv.at[c, most], recv_sem.at[way, c]).wait()

    def sent(way, c, send):
        pltpu.make_async_copy(send.at[c, most], send.at[c, most], send_sem.at[way, c]).wait()

    def gathered(recv, c, row):
        return jnp.concatenate(
            [
                jnp.concatenate(
                    [recv[c, pl.ds(row(part, b), SIDE, stride=PITCH), :] for b in range(3)], 1
                )
                for part in range(EACH)
            ],
            0,
        )

    lane = lax.broadcasted_iota(jnp.int32, (1, LANES), 1)

    def weight_of(c):
        weights = [mask_ref[i, c].astype(jnp.float32) for i in range(4)]
        return jnp.where(
            lane < 2 * N,
            jnp.where(lane < N, weights[0], weights[1]),
            jnp.where(lane < 3 * N, weights[2], weights[3]),
        )

    def along_x(c):
        weight = weight_of(c)

        def row_step(k, _):
            value = gathered(recv1, c, lambda p, b: chunk_row(p, k, b))
            spectrum = left(x_into_ref[...], value)
            value = spectrum * coulomb[k]
            for d in range(4):
                product = value * turned(spectrum, d)
                total = product[:8]
                for r in range(8, N, 8):
                    total = total + product[r : r + 8]
                gram[d] += total * weight
            value = left(x_out_ref[...], value)
            for p in range(EACH):
                for b in range(3):
                    send2[c, pl.ds(chunk_row(p, k, b), SIDE, stride=PITCH), :] = value[
                        p * SIDE : (p + 1) * SIDE, b * 128 : (b + 1) * 128
                    ]
            return 0

        lax.fori_loop(0, EACH, row_step, 0)

    def fields(c):
        weight = weight_of(c)

        def plane_step(p, _):
            value = gathered(recv2, c, lambda k, b: chunk_row(p, k, b))
            value = left(y_into_ref[...], value)
            value = right(value, zh_ref[...], zl_ref[...])
            term = value * rep[c, p] * weight
            field[p] = field[p] - term
            return 0

        lax.fori_loop(0, EACH, plane_step, 0)

    def prepare(p, _):
        own[p] = side_by_side(orb_ref, p)
        return 0

    lax.fori_loop(0, EACH, prepare, 0)
    pl.semaphore_wait(barrier, SIDE)
    passing(0).start()
    gram[...] = jnp.zeros_like(gram)
    field[...] = jnp.zeros_like(field)
    coul = BOX * BOX / math.pi / (N * N * N)
    for k in range(EACH):
        ky = me * EACH + k
        folded = jnp.where(ky * 2 >= N, ky - N, ky).astype(jnp.float32)
        squares = sq_ref[...] + folded * folded
        coulomb[k] = jnp.where(squares > 0.5, coul / jnp.maximum(squares, 1.0), 0.0)

    def turn(c, _):
        @pl.when(c < CHUNKS)
        def _():
            passing(c).wait_recv()

            @pl.when(c + 1 < CHUNKS)
            def _():
                passing(c + 1).start()

            densities(c)
            exchange(0, c, send1, recv1)

        @pl.when(c > 0)
        def _():
            arrived(0, c - 1, send1, recv1)
            along_x(c - 1)
            exchange(1, c - 1, send2, recv2)

        return 0

    lax.fori_loop(0, CHUNKS + 1, turn, 0)
    sums = [jnp.sum(gram[d], axis=0, keepdims=True) for d in range(4)]
    sums = jnp.concatenate(sums + [jnp.zeros((4, LANES), jnp.float32)], 0)
    high = sums.astype(jnp.bfloat16)
    middle, low = split(sums - high.astype(jnp.float32))
    pick = pick_ref[...]
    sums = dot(high, pick) + dot(middle, pick) + dot(low, pick)
    part_send[...] = sums
    part_recv[me] = sums

    def tell(t, _):
        pltpu.make_async_remote_copy(
            src_ref=part_send,
            dst_ref=part_recv.at[me],
            send_sem=part_sems.at[0],
            recv_sem=part_sems.at[1],
            device_id={"grid": (me + t) % SIDE},
            device_id_type=MESH,
        ).start()
        return 0

    lax.fori_loop(1, SIDE, tell, 0)

    def finish(c, _):
        arrived(1, c, send2, recv2)
        fields(c)
        return 0

    lax.fori_loop(0, CHUNKS, finish, 0)

    def lay_out(p, _):
        tiles = [
            [field[p, 24 * u : 24 * u + 24, 128 * t : 128 * t + 128] for t in range(3)]
            for u in range(4)
        ]
        for i in range(4):
            rows = joined([taken(tiles[u], i) for u in range(4)])
            for t in range(3):
                field_ref[i, pl.ds(p * PLANE + t, 24, stride=3), :] = rows[t]
        return 0

    lax.fori_loop(0, EACH, lay_out, 0)
    for c in range(CHUNKS):
        passing(c).wait_send()
        sent(0, c, send1)
        sent(1, c, send2)
    others = part_recv.at[pl.ds(0, SIDE - 1)]
    pltpu.make_async_copy(others, others, part_sems.at[1]).wait()
    pltpu.make_async_copy(others, others, part_sems.at[0]).wait()
    sums = jnp.sum(part_recv[...], axis=0) * (-1.0 / (N * N * N))
    apart = lax.broadcasted_iota(jnp.int32, (8, 128), 0) - lax.broadcasted_iota(jnp.int32, (8, 128), 1)
    result = jnp.zeros((8, 128), jnp.float32)
    for d in range(4):
        result = jnp.where((apart + 128) % 4 == d, sums[d : d + 1], result)
    proj_ref[...] = result


def vmem(count):
    return [pl.BlockSpec(memory_space=pltpu.VMEM)] * count


def at_distance(distance, mask, orbitals, *constants):
    def scratch(*shape):
        return pltpu.VMEM(shape, jnp.float32)

    buffer = scratch(CHUNKS, SIDE * PITCH, 128)
    return pl.pallas_call(
        functools.partial(body, distance),
        out_shape=(
            jax.ShapeDtypeStruct((4, FLAT, 128), jnp.float32),
            jax.ShapeDtypeStruct((8, 128), jnp.float32),
        ),
        in_specs=[pl.BlockSpec(memory_space=pltpu.SMEM)] + vmem(1 + len(constants)),
        out_specs=tuple(vmem(2)),
        scratch_shapes=[
            scratch(4, FLAT, 128),
            scratch(EACH, N, LANES),
            scratch(4, 8, LANES),
            scratch(4, EACH, N, LANES),
            scratch(EACH, N, LANES),
            scratch(EACH, N, LANES),
            buffer, buffer, buffer, buffer,
            scratch(8, 128),
            scratch(SIDE, 8, 128),
            pltpu.SemaphoreType.DMA((2, CHUNKS)),
            pltpu.SemaphoreType.DMA((2, CHUNKS)),
            pltpu.SemaphoreType.DMA((2, CHUNKS)),
            pltpu.SemaphoreType.DMA((2, CHUNKS)),
            pltpu.SemaphoreType.DMA((2,)),
        ],
        compiler_params=pltpu.CompilerParams(
            collective_id=distance - 1, has_side_effects=True, vmem_limit_bytes=40 * 1024 * 1024
        ),
        name=f"exchange_{distance}",
    )(mask, orbitals, *constants)


def shards(orbitals, pair_mask, cycle_step):
    constants = [jnp.asarray(t) for t in tables()]
    field, projection = lax.switch(
        cycle_step - 1,
        [functools.partial(at_distance, d) for d in range(1, BANDS)],
        pair_mask,
        orbitals.reshape(4, FLAT, 128),
        *constants,
    )
    return field.reshape(4, EACH, N * N), projection[:4, :4]


def solution(mesh):
    return jax.shard_map(
        shards,
        mesh=mesh,
        in_specs=(P("band", "grid", None), P("band", None), P()),
        out_specs=(P("band", "grid", None), P("band", None)),
        check_vma=False,
    )
```

```python
import functools
import math

import jax
import jax.numpy as jnp
import numpy as np
from jax import lax
from jax.experimental import pallas as pl
from jax.experimental.pallas import tpu as pltpu
from jax.sharding import PartitionSpec as P

N = 96
LANES = 4 * N
BOX = 16.0
SIDE = 32
EACH = 3
CHUNKS = 4
UNITS = CHUNKS * EACH
ROWS = EACH * 3
ROOM = 16
PITCH = EACH * ROOM
AHEAD = 4
X_AFTER = 6
Y_AFTER = 12
PLANE = N * N // 128
FLAT = EACH * PLANE
BANDS = 8
MESH = pl.DeviceIdType.MESH


def hartley():
    index = np.arange(N)
    angle = (index[:, None] * index[None, :] % N) * (2.0 * math.pi / N)
    return np.cos(angle) + np.sin(angle)


def two_parts(table):
    high = table.astype(jnp.bfloat16)
    low = (table - high.astype(np.float64)).astype(jnp.bfloat16)
    return high, low


def stacked(table):
    high, low = two_parts(table)
    return np.concatenate([np.concatenate([high, high], 1), np.concatenate([low, low], 1)], 0)


def tables():
    cas = hartley()
    order = np.array([EACH * (r % SIDE) + r // SIDE for r in range(N)])
    lines = np.array([4 * (r % 24) + r // 24 for r in range(N)])
    y_out = stacked(cas[order][:, lines])
    y_into = stacked(cas[lines][:, order])
    x_into = stacked(cas[:, order])
    x_out = stacked(cas[order])
    z_high, z_low = two_parts(np.kron(np.eye(4), cas))
    freq = np.arange(N)
    freq = np.where(freq * 2 >= N, freq - N, freq).astype(np.float32)
    squares = freq[:, None] ** 2 + np.tile(freq, 4)[None, :] ** 2
    pick = np.zeros((LANES, 128), np.float32)
    pick[np.arange(LANES), np.arange(LANES) // N] = 1.0
    pick = pick.astype(jnp.bfloat16)
    return y_out, y_into, x_into, x_out, z_high, z_low, squares.astype(np.float32), pick


def split(value):
    high = value.astype(jnp.bfloat16)
    low = (value - high.astype(jnp.float32)).astype(jnp.bfloat16)
    return high, low


def dot(a, b):
    return jnp.dot(a, b, preferred_element_type=jnp.float32)


def left(table, value):
    high, low = split(value)
    both = dot(table, jnp.concatenate([high, low], 0))
    return both[:N] + both[N:]


def right(value, z_high, z_low):
    high, low = split(value)
    rows = value.shape[0]
    both = dot(jnp.concatenate([high, low], 0), z_high)
    return both[:rows] + both[rows:] + dot(high, z_low)


def roll(value, shift):
    return pltpu.roll(value, shift, 1)


def lane_of(value):
    return lax.broadcasted_iota(jnp.int32, value.shape, 1)


def taken(tiles, j):
    a, b, c = tiles
    lane = lane_of(a)
    if j == 0:
        return a
    if j == 1:
        return jnp.where(lane < 32, roll(a, 32), roll(b, 32))
    if j == 2:
        return jnp.where(lane < 64, roll(b, 64), roll(c, 64))
    return roll(c, 96)


def joined(four):
    lane = lane_of(four[0])
    one, two = roll(four[1], 96), roll(four[2], 64)
    return [
        jnp.where(lane < 96, four[0], one),
        jnp.where(lane < 64, one, two),
        jnp.where(lane < 32, two, roll(four[3], 32)),
    ]


def turned(value, d):
    if d == 0:
        return value
    tiles = lane_tiles(value)
    rolled = [roll(t, 32 * d) for t in tiles]
    lane = lane_of(tiles[0])
    first = {1: 0, 2: 1, 3: 2}[d]
    return jnp.concatenate(
        [
            jnp.where(lane < 32 * d, rolled[(t + first) % 3], rolled[(t + first + 1) % 3])
            for t in range(3)
        ],
        1,
    )


def lane_tiles(value):
    return [value[:, 128 * t : 128 * t + 128] for t in range(3)]


def rows_of(ref, j, p):
    return [ref[j, pl.ds(p * PLANE + t, 24, stride=3), :] for t in range(3)]


def repeated(ref, j, p):
    tiles = rows_of(ref, j, p)
    lines = []
    for u in range(4):
        v = taken(tiles, u)
        lines.append(jnp.concatenate(joined([v, v, v, v]), 1))
    return jnp.concatenate(lines, 0)


def side_by_side(ref, p):
    tiles = [rows_of(ref, i, p) for i in range(4)]
    lines = []
    for u in range(4):
        lines.append(jnp.concatenate(joined([taken(tiles[i], u) for i in range(4)]), 1))
    return jnp.concatenate(lines, 0)


def body(
    distance,
    mask_ref, orb_ref, y_out_ref, y_into_ref, x_into_ref, x_out_ref, zh_ref, zl_ref, sq_ref, pick_ref,
    field_ref, proj_ref,
    vis, own, gram, rep, field, coulomb, send1, recv1, send2, recv2, part_send, part_recv,
    vis_sems, send_sem, recv_sem, own_sem, part_sems,
):
    me = lax.axis_index("grid")
    band = lax.axis_index("band")
    barrier = pltpu.get_barrier_semaphore()

    def greet(t, _):
        pl.semaphore_signal(barrier, inc=1, device_id={"grid": (me + t) % SIDE}, device_id_type=MESH)
        return 0

    source = (band + BANDS - distance) % BANDS
    pl.semaphore_signal(barrier, inc=1, device_id={"band": source}, device_id_type=MESH)
    lax.fori_loop(1, SIDE, greet, 0)

    def passing(n):
        plane = pl.ds(pl.multiple_of(n % EACH * PLANE, 8), PLANE)
        return pltpu.make_async_remote_copy(
            src_ref=orb_ref.at[n // EACH, plane],
            dst_ref=vis.at[n // EACH, plane],
            send_sem=vis_sems.at[0, n],
            recv_sem=vis_sems.at[1, n],
            device_id={"band": (band + distance) % BANDS},
            device_id_type=MESH,
        )

    def unit_row(unit, part, b):
        return unit * ROOM + part * 3 + b

    def densities(n):
        c, p = n // EACH, n % EACH
        visiting = repeated(vis, c, p)
        rep[c, p] = visiting
        value = right(own[p] * visiting, zh_ref[...], zl_ref[...])
        value = left(y_out_ref[...], value)
        spread(send1, c, p, value)

    def spread(send, c, unit, value):
        for part in range(EACH):
            for b in range(3):
                send[c, pl.ds(unit_row(unit, part, b), SIDE, stride=PITCH), :] = value[
                    part * SIDE : (part + 1) * SIDE, b * 128 : (b + 1) * 128
                ]

    def gathered(recv, c, row):
        return jnp.concatenate(
            [
                jnp.concatenate(
                    [recv[c, pl.ds(row(unit, b), SIDE, stride=PITCH), :] for b in range(3)], 1
                )
                for unit in range(EACH)
            ],
            0,
        )

    def rows_at(device, unit):
        return pl.ds(pl.multiple_of(device * PITCH + unit * ROOM, 8), ROWS)

    def exchange(way, n, send, recv):
        c, unit = n // EACH, n % EACH

        def one(t, _):
            to = (me + t) % SIDE
            pltpu.make_async_remote_copy(
                src_ref=send.at[c, rows_at(to, unit)],
                dst_ref=recv.at[c, rows_at(me, unit)],
                send_sem=send_sem.at[way, c],
                recv_sem=recv_sem.at[way, c],
                device_id={"grid": to},
                device_id_type=MESH,
            ).start()
            return 0

        lax.fori_loop(1, SIDE, one, 0)
        mine = rows_at(me, unit)
        pltpu.make_async_copy(send.at[c, mine], recv.at[c, mine], own_sem.at[way, c]).start()

    all_own = pl.ds(0, EACH * ROWS)
    all_others = pl.ds(0, (SIDE - 1) * EACH * ROWS)

    def arrived(way, c, recv):
        own_part, other_part = recv.at[c, all_own], recv.at[c, all_others]
        pltpu.make_async_copy(own_part, own_part, own_sem.at[way, c]).wait()
        pltpu.make_async_copy(other_part, other_part, recv_sem.at[way, c]).wait()

    def sent(way, c, send):
        part = send.at[c, all_others]
        pltpu.make_async_copy(part, part, send_sem.at[way, c]).wait()

    lane = lax.broadcasted_iota(jnp.int32, (1, LANES), 1)

    def weight_of(c):
        weights = [mask_ref[i, c].astype(jnp.float32) for i in range(4)]
        return jnp.where(
            lane < 2 * N,
            jnp.where(lane < N, weights[0], weights[1]),
            jnp.where(lane < 3 * N, weights[2], weights[3]),
        )

    def along_x(n):
        c, k = n // EACH, n % EACH
        weight = weight_of(c)
        value = gathered(recv1, c, lambda p, b: unit_row(p, k, b))
        spectrum = left(x_into_ref[...], value)
        value = spectrum * coulomb[k]
        for d in range(4):
            product = value * turned(spectrum, d)
            total = product[:8]
            for r in range(8, N, 8):
                total = total + product[r : r + 8]
            gram[d] += total * weight
        value = left(x_out_ref[...], value)
        spread(send2, c, k, value)

    def fields(n):
        c, p = n // EACH, n % EACH
        value = gathered(recv2, c, lambda k, b: unit_row(k, p, b))
        value = left(y_into_ref[...], value)
        value = right(value, zh_ref[...], zl_ref[...])
        field[p] = field[p] - value * rep[c, p] * weight_of(c)

    def prepare(p, _):
        own[p] = side_by_side(orb_ref, p)
        return 0

    lax.fori_loop(0, EACH, prepare, 0)
    pl.semaphore_wait(barrier, SIDE)
    for n in range(AHEAD):
        passing(n).start()
    gram[...] = jnp.zeros_like(gram)
    field[...] = jnp.zeros_like(field)
    coul = BOX * BOX / math.pi / (N * N * N)
    for k in range(EACH):
        ky = me * EACH + k
        folded = jnp.where(ky * 2 >= N, ky - N, ky).astype(jnp.float32)
        squares = sq_ref[...] + folded * folded
        coulomb[k] = jnp.where(squares > 0.5, coul / jnp.maximum(squares, 1.0), 0.0)

    def tell_sums():
        sums = [jnp.sum(gram[d], axis=0, keepdims=True) for d in range(4)]
        sums = jnp.concatenate(sums + [jnp.zeros((4, LANES), jnp.float32)], 0)
        high = sums.astype(jnp.bfloat16)
        middle, low = split(sums - high.astype(jnp.float32))
        pick = pick_ref[...]
        sums = dot(high, pick) + dot(middle, pick) + dot(low, pick)
        part_send[...] = sums
        part_recv[me] = sums

        def tell(t, _):
            pltpu.make_async_remote_copy(
                src_ref=part_send,
                dst_ref=part_recv.at[me],
                send_sem=part_sems.at[0],
                recv_sem=part_sems.at[1],
                device_id={"grid": (me + t) % SIDE},
                device_id_type=MESH,
            ).start()
            return 0

        lax.fori_loop(1, SIDE, tell, 0)

    def turn(n, _):
        @pl.when(n < UNITS)
        def _():
            passing(n).wait_recv()

            @pl.when(n + AHEAD < UNITS)
            def _():
                passing(n + AHEAD).start()

            densities(n)
            exchange(0, n, send1, recv1)

        m = n - X_AFTER

        @pl.when((m >= 0) & (m < UNITS))
        def _():
            @pl.when(m % EACH == 0)
            def _():
                arrived(0, m // EACH, recv1)

            along_x(m)
            exchange(1, m, send2, recv2)

        @pl.when(m == UNITS - 1)
        def _():
            tell_sums()

        f = n - Y_AFTER

        @pl.when(f >= 0)
        def _():
            @pl.when(f % EACH == 0)
            def _():
                arrived(1, f // EACH, recv2)

            fields(f)

        return 0

    lax.fori_loop(0, UNITS + Y_AFTER, turn, 0)

    def lay_out(p, _):
        tiles = [
            [field[p, 24 * u : 24 * u + 24, 128 * t : 128 * t + 128] for t in range(3)]
            for u in range(4)
        ]
        for i in range(4):
            rows = joined([taken(tiles[u], i) for u in range(4)])
            for t in range(3):
                field_ref[i, pl.ds(p * PLANE + t, 24, stride=3), :] = rows[t]
        return 0

    lax.fori_loop(0, EACH, lay_out, 0)
    for n in range(UNITS):
        passing(n).wait_send()
    for c in range(CHUNKS):
        sent(0, c, send1)
        sent(1, c, send2)
    others = part_recv.at[pl.ds(0, SIDE - 1)]
    pltpu.make_async_copy(others, others, part_sems.at[1]).wait()
    pltpu.make_async_copy(others, others, part_sems.at[0]).wait()
    sums = jnp.sum(part_recv[...], axis=0) * (-1.0 / (N * N * N))
    apart = lax.broadcasted_iota(jnp.int32, (8, 128), 0) - lax.broadcasted_iota(jnp.int32, (8, 128), 1)
    result = jnp.zeros((8, 128), jnp.float32)
    for d in range(4):
        result = jnp.where((apart + 128) % 4 == d, sums[d : d + 1], result)
    proj_ref[...] = result


def vmem(count):
    return [pl.BlockSpec(memory_space=pltpu.VMEM)] * count


def at_distance(distance, mask, orbitals, *constants):
    def scratch(*shape):
        return pltpu.VMEM(shape, jnp.float32)

    buffer = scratch(CHUNKS, SIDE * PITCH, 128)
    return pl.pallas_call(
        functools.partial(body, distance),
        out_shape=(
            jax.ShapeDtypeStruct((4, FLAT, 128), jnp.float32),
            jax.ShapeDtypeStruct((8, 128), jnp.float32),
        ),
        in_specs=[pl.BlockSpec(memory_space=pltpu.SMEM)] + vmem(1 + len(constants)),
        out_specs=tuple(vmem(2)),
        scratch_shapes=[
            scratch(4, FLAT, 128),
            scratch(EACH, N, LANES),
            scratch(4, 8, LANES),
            scratch(4, EACH, N, LANES),
            scratch(EACH, N, LANES),
            scratch(EACH, N, LANES),
            buffer, buffer, buffer, buffer,
            scratch(8, 128),
            scratch(SIDE, 8, 128),
            pltpu.SemaphoreType.DMA((2, UNITS)),
            pltpu.SemaphoreType.DMA((2, CHUNKS)),
            pltpu.SemaphoreType.DMA((2, CHUNKS)),
            pltpu.SemaphoreType.DMA((2, CHUNKS)),
            pltpu.SemaphoreType.DMA((2,)),
        ],
        compiler_params=pltpu.CompilerParams(
            collective_id=distance - 1, has_side_effects=True, vmem_limit_bytes=40 * 1024 * 1024
        ),
        name=f"exchange_{distance}",
    )(mask, orbitals, *constants)


def shards(orbitals, pair_mask, cycle_step):
    constants = [jnp.asarray(t) for t in tables()]
    field, projection = lax.switch(
        cycle_step - 1,
        [functools.partial(at_distance, d) for d in range(1, BANDS)],
        pair_mask,
        orbitals.reshape(4, FLAT, 128),
        *constants,
    )
    return field.reshape(4, EACH, N * N), projection[:4, :4]


def solution(mesh):
    return jax.shard_map(
        shards,
        mesh=mesh,
        in_specs=(P("band", "grid", None), P("band", None), P()),
        out_specs=(P("band", "grid", None), P("band", None)),
        check_vma=False,
    )
```

```python
import functools
import math

import jax
import jax.numpy as jnp
import numpy as np
from jax import lax
from jax.experimental import pallas as pl
from jax.experimental.pallas import tpu as pltpu
from jax.sharding import PartitionSpec as P

N = 96
LANES = 4 * N
BOX = 16.0
SIDE = 32
EACH = 3
CHUNKS = 4
UNITS = CHUNKS * EACH
ROWS = EACH * 3
ROOM = 16
PITCH = EACH * ROOM + 8
AHEAD = 4
VIA = 2
X_AFTER = 6
Y_AFTER = 12
PLANE = N * N // 128
FLAT = EACH * PLANE
BANDS = 8
MESH = pl.DeviceIdType.MESH


def hartley():
    index = np.arange(N)
    angle = (index[:, None] * index[None, :] % N) * (2.0 * math.pi / N)
    return np.cos(angle) + np.sin(angle)


def two_parts(table):
    high = table.astype(jnp.bfloat16)
    low = (table - high.astype(np.float64)).astype(jnp.bfloat16)
    return high, low


def stacked(table):
    high, low = two_parts(table)
    return np.concatenate([np.concatenate([high, high], 1), np.concatenate([low, low], 1)], 0)


def tables():
    cas = hartley()
    order = np.array([EACH * (r % SIDE) + r // SIDE for r in range(N)])
    lines = np.array([4 * (r % 24) + r // 24 for r in range(N)])
    y_out = stacked(cas[order][:, lines])
    y_into = stacked(cas[lines][:, order])
    x_into = stacked(cas[:, order])
    x_out = stacked(cas[order])
    z_high, z_low = two_parts(np.kron(np.eye(4), cas))
    freq = np.arange(N)
    freq = np.where(freq * 2 >= N, freq - N, freq).astype(np.float32)
    squares = freq[:, None] ** 2 + np.tile(freq, 4)[None, :] ** 2
    pick = np.zeros((LANES, 128), np.float32)
    pick[np.arange(LANES), np.arange(LANES) // N] = 1.0
    pick = pick.astype(jnp.bfloat16)
    return y_out, y_into, x_into, x_out, z_high, z_low, squares.astype(np.float32), pick


def split(value):
    high = value.astype(jnp.bfloat16)
    low = (value - high.astype(jnp.float32)).astype(jnp.bfloat16)
    return high, low


def dot(a, b):
    return jnp.dot(a, b, preferred_element_type=jnp.float32)


def left(table, value):
    high, low = split(value)
    both = dot(table, jnp.concatenate([high, low], 0))
    return both[:N] + both[N:]


def right(value, z_high, z_low):
    high, low = split(value)
    rows = value.shape[0]
    both = dot(jnp.concatenate([high, low], 0), z_high)
    return both[:rows] + both[rows:] + dot(high, z_low)


def roll(value, shift):
    return pltpu.roll(value, shift, 1)


def lane_of(value):
    return lax.broadcasted_iota(jnp.int32, value.shape, 1)


def taken(tiles, j):
    a, b, c = tiles
    lane = lane_of(a)
    if j == 0:
        return a
    if j == 1:
        return jnp.where(lane < 32, roll(a, 32), roll(b, 32))
    if j == 2:
        return jnp.where(lane < 64, roll(b, 64), roll(c, 64))
    return roll(c, 96)


def joined(four):
    lane = lane_of(four[0])
    one, two = roll(four[1], 96), roll(four[2], 64)
    return [
        jnp.where(lane < 96, four[0], one),
        jnp.where(lane < 64, one, two),
        jnp.where(lane < 32, two, roll(four[3], 32)),
    ]


def turned(value, d):
    if d == 0:
        return value
    tiles = lane_tiles(value)
    rolled = [roll(t, 32 * d) for t in tiles]
    lane = lane_of(tiles[0])
    first = {1: 0, 2: 1, 3: 2}[d]
    return jnp.concatenate(
        [
            jnp.where(lane < 32 * d, rolled[(t + first) % 3], rolled[(t + first + 1) % 3])
            for t in range(3)
        ],
        1,
    )


def lane_tiles(value):
    return [value[:, 128 * t : 128 * t + 128] for t in range(3)]


def rows_of(ref, j, p):
    return [ref[j, pl.ds(p * PLANE + t, 24, stride=3), :] for t in range(3)]


def repeated(ref, j, p):
    tiles = rows_of(ref, j, p)
    lines = []
    for u in range(4):
        v = taken(tiles, u)
        lines.append(jnp.concatenate(joined([v, v, v, v]), 1))
    return jnp.concatenate(lines, 0)


def side_by_side(ref, p):
    tiles = [rows_of(ref, i, p) for i in range(4)]
    lines = []
    for u in range(4):
        lines.append(jnp.concatenate(joined([taken(tiles[i], u) for i in range(4)]), 1))
    return jnp.concatenate(lines, 0)


def body(
    distance,
    mask_ref, orb_hbm, *refs,
):
    tables_hbm, refs = refs[:8], refs[8:]
    field_ref, proj_ref, orb_ref = refs[:3]
    table_refs, refs = refs[3:11], refs[11:]
    y_out_ref, y_into_ref, x_into_ref, x_out_ref, zh_ref, zl_ref, sq_ref, pick_ref = table_refs
    vis, relay, own, gram, rep, field, coulomb, send1, recv1, send2, recv2, part_send, part_recv = refs[:13]
    vis_sems, relay_sems, send_sem, recv_sem, own_sem, part_sems, load_sems = refs[13:]
    me = lax.axis_index("grid")
    band = lax.axis_index("band")
    barrier = pltpu.get_barrier_semaphore()

    def greet(t, _):
        pl.semaphore_signal(barrier, inc=1, device_id={"grid": (me + t) % SIDE}, device_id_type=MESH)
        return 0

    def at_band(hops):
        return {"band": (band + hops + BANDS) % BANDS}

    split_ways = distance in (3, 5)
    way_on = 1 if distance == 3 else -1
    sources = [-distance]
    if split_ways:
        sources += [VIA * way_on, (BANDS - 3 - VIA) * way_on]
    for hops in sources:
        pl.semaphore_signal(barrier, inc=1, device_id=at_band(hops), device_id_type=MESH)
    lax.fori_loop(1, SIDE, greet, 0)

    def loading(n):
        return pltpu.make_async_copy(
            orb_hbm.at[n % EACH, :, n // EACH, :],
            orb_ref.at[n // EACH, pl.ds(n % EACH * PLANE, PLANE)],
            load_sems.at[n],
        )

    table_loads = [
        pltpu.make_async_copy(tables_hbm[t], table_refs[t], load_sems.at[UNITS + t]) for t in range(8)
    ]
    for n in range(UNITS):
        loading(n).start()
    for load in table_loads:
        load.start()

    def plane_of(n):
        return pl.ds(pl.multiple_of(n % EACH * PLANE, 8), PLANE)

    def passing(n):
        return pltpu.make_async_remote_copy(
            src_ref=orb_ref.at[n // EACH, plane_of(n)],
            dst_ref=vis.at[n // EACH, plane_of(n)],
            send_sem=vis_sems.at[0, n],
            recv_sem=vis_sems.at[1, n],
            device_id=at_band(distance),
            device_id_type=MESH,
        )

    def first_leg(i):
        return pltpu.make_async_remote_copy(
            src_ref=orb_ref.at[i, plane_of(EACH - 1)],
            dst_ref=relay.at[i],
            send_sem=relay_sems.at[0, i],
            recv_sem=relay_sems.at[1, i],
            device_id=at_band(-VIA * way_on),
            device_id_type=MESH,
        )

    def second_leg(i):
        return pltpu.make_async_remote_copy(
            src_ref=relay.at[i],
            dst_ref=vis.at[i, plane_of(EACH - 1)],
            send_sem=relay_sems.at[2, i],
            recv_sem=vis_sems.at[1, EACH * i + EACH - 1],
            device_id=at_band((VIA + 3 - BANDS) * way_on),
            device_id_type=MESH,
        )

    def begin_passing():
        if split_ways:
            for i in range(2):
                for n in (EACH * i, EACH * i + 1):
                    passing(n).start()
                first_leg(i).start()
        else:
            for n in range(AHEAD):
                passing(n).start()

    def pass_on(n):
        if not split_ways:

            @pl.when(n + AHEAD < UNITS)
            def _():
                passing(n + AHEAD).start()

            return

        @pl.when((n % EACH != EACH - 1) & (n + 2 * EACH < UNITS))
        def _():
            passing(n + 2 * EACH).start()

        @pl.when((n % EACH == EACH - 1) & (n + 2 * EACH < UNITS))
        def _():
            first_leg(n // EACH + 2).start()

        @pl.when(n % EACH == 0)
        def _():
            first_leg(n // EACH).wait_recv()
            second_leg(n // EACH).start()

    def end_passing():
        for n in range(UNITS):
            if split_ways and n % EACH == EACH - 1:
                first_leg(n // EACH).wait_send()
                second_leg(n // EACH).wait_send()
            else:
                passing(n).wait_send()

    def unit_row(unit, part, b):
        return unit * ROOM + part * 3 + b

    def densities(n):
        c, p = n // EACH, n % EACH
        visiting = repeated(vis, c, p)
        rep[c, p] = visiting
        value = right(own[p] * visiting, zh_ref[...], zl_ref[...])
        value = left(y_out_ref[...], value)
        spread(send1, c, p, value)

    def spread(send, c, unit, value):
        for part in range(EACH):
            for b in range(3):
                send[c, pl.ds(unit_row(unit, part, b), SIDE, stride=PITCH), :] = value[
                    part * SIDE : (part + 1) * SIDE, b * 128 : (b + 1) * 128
                ]

    def gathered(recv, c, row):
        return jnp.concatenate(
            [
                jnp.concatenate(
                    [recv[c, pl.ds(row(unit, b), SIDE, stride=PITCH), :] for b in range(3)], 1
                )
                for unit in range(EACH)
            ],
            0,
        )

    def rows_at(device, unit):
        return pl.ds(pl.multiple_of(device * PITCH + unit * ROOM, 8), ROWS)

    def exchange(way, n, send, recv):
        c, unit = n // EACH, n % EACH

        def one(t, _):
            to = (me + t) % SIDE
            pltpu.make_async_remote_copy(
                src_ref=send.at[c, rows_at(to, unit)],
                dst_ref=recv.at[c, rows_at(me, unit)],
                send_sem=send_sem.at[way, c],
                recv_sem=recv_sem.at[way, c],
                device_id={"grid": to},
                device_id_type=MESH,
            ).start()
            return 0

        lax.fori_loop(1, SIDE, one, 0)
        mine = rows_at(me, unit)
        pltpu.make_async_copy(send.at[c, mine], recv.at[c, mine], own_sem.at[way, c]).start()

    all_own = pl.ds(0, EACH * ROWS)
    all_others = pl.ds(0, (SIDE - 1) * EACH * ROWS)

    def arrived(way, c, recv):
        own_part, other_part = recv.at[c, all_own], recv.at[c, all_others]
        pltpu.make_async_copy(own_part, own_part, own_sem.at[way, c]).wait()
        pltpu.make_async_copy(other_part, other_part, recv_sem.at[way, c]).wait()

    def sent(way, c, send):
        part = send.at[c, all_others]
        pltpu.make_async_copy(part, part, send_sem.at[way, c]).wait()

    lane = lax.broadcasted_iota(jnp.int32, (1, LANES), 1)

    def weight_of(c):
        weights = [mask_ref[i, c].astype(jnp.float32) for i in range(4)]
        return jnp.where(
            lane < 2 * N,
            jnp.where(lane < N, weights[0], weights[1]),
            jnp.where(lane < 3 * N, weights[2], weights[3]),
        )

    def along_x(n):
        c, k = n // EACH, n % EACH
        weight = weight_of(c)
        value = gathered(recv1, c, lambda p, b: unit_row(p, k, b))
        spectrum = left(x_into_ref[...], value)
        value = spectrum * coulomb[k]
        for d in range(4):
            product = value * turned(spectrum, d)
            total = product[:8]
            for r in range(8, N, 8):
                total = total + product[r : r + 8]
            gram[d] += total * weight
        value = left(x_out_ref[...], value)
        spread(send2, c, k, value)

    def fields(n):
        c, p = n // EACH, n % EACH
        value = gathered(recv2, c, lambda k, b: unit_row(k, p, b))
        value = left(y_into_ref[...], value)
        value = right(value, zh_ref[...], zl_ref[...])
        field[p] = field[p] - value * rep[c, p] * weight_of(c)

    def prepare(p, _):
        own[p] = side_by_side(orb_ref, p)
        return 0

    for n in range(UNITS):
        loading(n).wait()
    pl.semaphore_wait(barrier, SIDE - 1 + len(sources))
    begin_passing()
    lax.fori_loop(0, EACH, prepare, 0)
    for load in table_loads:
        load.wait()
    gram[...] = jnp.zeros_like(gram)
    field[...] = jnp.zeros_like(field)
    coul = BOX * BOX / math.pi / (N * N * N)
    for k in range(EACH):
        ky = me * EACH + k
        folded = jnp.where(ky * 2 >= N, ky - N, ky).astype(jnp.float32)
        squares = sq_ref[...] + folded * folded
        coulomb[k] = jnp.where(squares > 0.5, coul / jnp.maximum(squares, 1.0), 0.0)

    def tell_sums():
        sums = [jnp.sum(gram[d], axis=0, keepdims=True) for d in range(4)]
        sums = jnp.concatenate(sums + [jnp.zeros((4, LANES), jnp.float32)], 0)
        high = sums.astype(jnp.bfloat16)
        middle, low = split(sums - high.astype(jnp.float32))
        pick = pick_ref[...]
        sums = dot(high, pick) + dot(middle, pick) + dot(low, pick)
        part_send[...] = sums
        part_recv[me] = sums

        def tell(t, _):
            pltpu.make_async_remote_copy(
                src_ref=part_send,
                dst_ref=part_recv.at[me],
                send_sem=part_sems.at[0],
                recv_sem=part_sems.at[1],
                device_id={"grid": (me + t) % SIDE},
                device_id_type=MESH,
            ).start()
            return 0

        lax.fori_loop(1, SIDE, tell, 0)

    def storing(p, i):
        return pltpu.make_async_copy(
            vis.at[i, pl.ds(pl.multiple_of(p * PLANE, 8), PLANE)],
            field_ref.at[p, :, i, :],
            load_sems.at[p * 4 + i],
        )

    def lay_out(p):
        tiles = [
            [field[p, 24 * u : 24 * u + 24, 128 * t : 128 * t + 128] for t in range(3)]
            for u in range(4)
        ]
        for i in range(4):
            rows = joined([taken(tiles[u], i) for u in range(4)])
            for t in range(3):
                vis[i, pl.ds(p * PLANE + t, 24, stride=3), :] = rows[t]
        for i in range(4):
            storing(p, i).start()

    def turn(n, _):
        @pl.when(n < UNITS)
        def _():
            passing(n).wait_recv()

            pass_on(n)
            densities(n)
            exchange(0, n, send1, recv1)

        m = n - X_AFTER

        @pl.when((m >= 0) & (m < UNITS))
        def _():
            @pl.when(m % EACH == 0)
            def _():
                arrived(0, m // EACH, recv1)

            along_x(m)
            exchange(1, m, send2, recv2)

        @pl.when(m == UNITS - 1)
        def _():
            tell_sums()

        f = n - Y_AFTER

        @pl.when(f >= 0)
        def _():
            @pl.when(f % EACH == 0)
            def _():
                arrived(1, f // EACH, recv2)

            fields(f)

        @pl.when(f >= UNITS - EACH)
        def _():
            lay_out(f % EACH)

        return 0

    lax.fori_loop(0, UNITS + Y_AFTER, turn, 0)

    end_passing()
    for c in range(CHUNKS):
        sent(0, c, send1)
        sent(1, c, send2)
    others = part_recv.at[pl.ds(0, SIDE - 1)]
    pltpu.make_async_copy(others, others, part_sems.at[1]).wait()
    pltpu.make_async_copy(others, others, part_sems.at[0]).wait()
    sums = jnp.sum(part_recv[...], axis=0) * (-1.0 / (N * N * N))
    apart = lax.broadcasted_iota(jnp.int32, (8, 128), 0) - lax.broadcasted_iota(jnp.int32, (8, 128), 1)
    result = jnp.zeros((8, 128), jnp.float32)
    for d in range(4):
        result = jnp.where((apart + 128) % 4 == d, sums[d : d + 1], result)
    proj_ref[...] = result[:4, :4]
    for n in range(UNITS):
        storing(n // 4, n % 4).wait()


def vmem(count):
    return [pl.BlockSpec(memory_space=pltpu.VMEM)] * count


def at_distance(distance, mask, orbitals, *constants):
    def scratch(*shape):
        return pltpu.VMEM(shape, jnp.float32)

    buffer = scratch(CHUNKS, SIDE * PITCH, 128)
    return pl.pallas_call(
        functools.partial(body, distance),
        out_shape=(
            jax.ShapeDtypeStruct((EACH, PLANE, 4, 128), jnp.float32),
            jax.ShapeDtypeStruct((4, 4), jnp.float32),
        ),
        in_specs=[pl.BlockSpec(memory_space=pltpu.SMEM)]
        + [pl.BlockSpec(memory_space=pltpu.HBM)] * (1 + len(constants)),
        out_specs=tuple(vmem(2)),
        scratch_shapes=[
            scratch(4, FLAT, 128),
            *[pltpu.VMEM(table.shape, table.dtype) for table in constants],
            scratch(4, FLAT, 128),
            scratch(4, PLANE, 128),
            scratch(EACH, N, LANES),
            scratch(4, 8, LANES),
            scratch(4, EACH, N, LANES),
            scratch(EACH, N, LANES),
            scratch(EACH, N, LANES),
            buffer, buffer, buffer, buffer,
            scratch(8, 128),
            scratch(SIDE, 8, 128),
            pltpu.SemaphoreType.DMA((2, UNITS)),
            pltpu.SemaphoreType.DMA((3, 4)),
            pltpu.SemaphoreType.DMA((2, CHUNKS)),
            pltpu.SemaphoreType.DMA((2, CHUNKS)),
            pltpu.SemaphoreType.DMA((2, CHUNKS)),
            pltpu.SemaphoreType.DMA((2,)),
            pltpu.SemaphoreType.DMA((UNITS + 8,)),
        ],
        compiler_params=pltpu.CompilerParams(
            collective_id=distance - 1, has_side_effects=True, vmem_limit_bytes=40 * 1024 * 1024
        ),
        name=f"exchange_{distance}",
    )(mask, orbitals, *constants)


def shards(orbitals, pair_mask, cycle_step):
    constants = [jnp.asarray(t) for t in tables()]
    field, projection = lax.switch(
        cycle_step - 1,
        [functools.partial(at_distance, d) for d in range(1, BANDS)],
        pair_mask,
        orbitals.reshape(4, EACH, PLANE, 128).transpose(1, 2, 0, 3),
        *constants,
    )
    return field.transpose(2, 0, 1, 3).reshape(4, EACH, N * N), projection


def solution(mesh):
    return jax.shard_map(
        shards,
        mesh=mesh,
        in_specs=(P("band", "grid", None), P("band", None), P()),
        out_specs=(P("band", "grid", None), P("band", None)),
        check_vma=False,
    )
```

```python
import functools
import math

import jax
import jax.numpy as jnp
import numpy as np
from jax import lax
from jax.experimental import pallas as pl
from jax.experimental.pallas import tpu as pltpu
from jax.sharding import PartitionSpec as P

N = 96
LANES = 4 * N
BOX = 16.0
SIDE = 32
EACH = 3
CHUNKS = 4
UNITS = CHUNKS * EACH
ROWS = EACH * 3
ROOM = 16
PITCH = EACH * ROOM + 8
AHEAD = 4
VIA = 2
X_AFTER = 6
Y_AFTER = 12
PLANE = N * N // 128
FLAT = EACH * PLANE
BANDS = 8
MESH = pl.DeviceIdType.MESH


def hartley():
    index = np.arange(N)
    angle = (index[:, None] * index[None, :] % N) * (2.0 * math.pi / N)
    return np.cos(angle) + np.sin(angle)


def two_parts(table):
    high = table.astype(jnp.bfloat16)
    low = (table - high.astype(np.float64)).astype(jnp.bfloat16)
    return high, low


def stacked(table):
    high, low = two_parts(table)
    return np.concatenate([np.concatenate([high, high], 1), np.concatenate([low, low], 1)], 0)


def tables():
    cas = hartley()
    order = np.array([EACH * (r % SIDE) + r // SIDE for r in range(N)])
    lines = np.array([4 * (r % 24) + r // 24 for r in range(N)])
    y_out = stacked(cas[order][:, lines])
    y_into = stacked(cas[lines][:, order])
    x_into = stacked(cas[:, order])
    x_out = stacked(cas[order])
    z_high, z_low = two_parts(np.kron(np.eye(4), cas))
    freq = np.arange(N)
    freq = np.where(freq * 2 >= N, freq - N, freq).astype(np.float32)
    squares = freq[:, None] ** 2 + np.tile(freq, 4)[None, :] ** 2
    pick = np.zeros((LANES, 128), np.float32)
    pick[np.arange(LANES), np.arange(LANES) // N] = 1.0
    pick = pick.astype(jnp.bfloat16)
    return y_out, y_into, x_into, x_out, z_high, z_low, squares.astype(np.float32), pick


def split(value):
    high = value.astype(jnp.bfloat16)
    low = (value - high.astype(jnp.float32)).astype(jnp.bfloat16)
    return high, low


def dot(a, b):
    return jnp.dot(a, b, preferred_element_type=jnp.float32)


def left(table, value):
    high, low = split(value)
    both = dot(table, jnp.concatenate([high, low], 0))
    return both[:N] + both[N:]


def right(value, z_high, z_low):
    high, low = split(value)
    rows = value.shape[0]
    both = dot(jnp.concatenate([high, low], 0), z_high)
    return both[:rows] + both[rows:] + dot(high, z_low)


def roll(value, shift):
    return pltpu.roll(value, shift, 1)


def lane_of(value):
    return lax.broadcasted_iota(jnp.int32, value.shape, 1)


def taken(tiles, j):
    a, b, c = tiles
    lane = lane_of(a)
    if j == 0:
        return a
    if j == 1:
        return jnp.where(lane < 32, roll(a, 32), roll(b, 32))
    if j == 2:
        return jnp.where(lane < 64, roll(b, 64), roll(c, 64))
    return roll(c, 96)


def joined(four):
    lane = lane_of(four[0])
    one, two = roll(four[1], 96), roll(four[2], 64)
    return [
        jnp.where(lane < 96, four[0], one),
        jnp.where(lane < 64, one, two),
        jnp.where(lane < 32, two, roll(four[3], 32)),
    ]


def turned(value, d):
    if d == 0:
        return value
    tiles = lane_tiles(value)
    rolled = [roll(t, 32 * d) for t in tiles]
    lane = lane_of(tiles[0])
    first = {1: 0, 2: 1, 3: 2}[d]
    return jnp.concatenate(
        [
            jnp.where(lane < 32 * d, rolled[(t + first) % 3], rolled[(t + first + 1) % 3])
            for t in range(3)
        ],
        1,
    )


def lane_tiles(value):
    return [value[:, 128 * t : 128 * t + 128] for t in range(3)]


def rows_of(ref, j, p):
    return [ref[j, pl.ds(p * PLANE + t, 24, stride=3), :] for t in range(3)]


def repeated(ref, j, p):
    tiles = rows_of(ref, j, p)
    lines = []
    for u in range(4):
        v = taken(tiles, u)
        lines.append(jnp.concatenate(joined([v, v, v, v]), 1))
    return jnp.concatenate(lines, 0)


def side_by_side(ref, p):
    tiles = [rows_of(ref, i, p) for i in range(4)]
    lines = []
    for u in range(4):
        lines.append(jnp.concatenate(joined([taken(tiles[i], u) for i in range(4)]), 1))
    return jnp.concatenate(lines, 0)


def body(
    distance,
    mask_ref, orb_hbm, *refs,
):
    tables_hbm, refs = refs[:8], refs[8:]
    field_ref, proj_ref, orb_ref = refs[:3]
    table_refs, refs = refs[3:11], refs[11:]
    y_out_ref, y_into_ref, x_into_ref, x_out_ref, zh_ref, zl_ref, sq_ref, pick_ref = table_refs
    vis, relay, own, gram, rep, field, coulomb, send1, recv1, send2, recv2, part_send, part_recv = refs[:13]
    vis_sems, relay_sems, send_sem, recv_sem, own_sem, part_sems, load_sems = refs[13:]
    me = lax.axis_index("grid")
    band = lax.axis_index("band")
    barrier = pltpu.get_barrier_semaphore()

    def greet(t, _):
        pl.semaphore_signal(barrier, inc=1, device_id={"grid": (me + t) % SIDE}, device_id_type=MESH)
        return 0

    def at_band(hops):
        return {"band": (band + hops + BANDS) % BANDS}

    split_ways = distance in (3, 5)
    way_on = 1 if distance == 3 else -1
    sources = [-distance]
    if split_ways:
        sources += [VIA * way_on, (BANDS - 3 - VIA) * way_on]
    for hops in sources:
        pl.semaphore_signal(barrier, inc=1, device_id=at_band(hops), device_id_type=MESH)
    lax.fori_loop(1, SIDE, greet, 0)

    def loading(n):
        return pltpu.make_async_copy(
            orb_hbm.at[n % EACH, :, n // EACH, :],
            orb_ref.at[n // EACH, pl.ds(n % EACH * PLANE, PLANE)],
            load_sems.at[n],
        )

    table_loads = [
        pltpu.make_async_copy(tables_hbm[t], table_refs[t], load_sems.at[UNITS + t]) for t in range(8)
    ]
    for n in range(UNITS):
        loading(n).start()
    for load in table_loads:
        load.start()

    def plane_of(n):
        return pl.ds(pl.multiple_of(n % EACH * PLANE, 8), PLANE)

    def passing(n):
        return pltpu.make_async_remote_copy(
            src_ref=orb_ref.at[n // EACH, plane_of(n)],
            dst_ref=vis.at[n // EACH, plane_of(n)],
            send_sem=vis_sems.at[0, n],
            recv_sem=vis_sems.at[1, n],
            device_id=at_band(distance),
            device_id_type=MESH,
        )

    def first_leg(i):
        return pltpu.make_async_remote_copy(
            src_ref=orb_ref.at[i, plane_of(EACH - 1)],
            dst_ref=relay.at[i],
            send_sem=relay_sems.at[0, i],
            recv_sem=relay_sems.at[1, i],
            device_id=at_band(-VIA * way_on),
            device_id_type=MESH,
        )

    def second_leg(i):
        return pltpu.make_async_remote_copy(
            src_ref=relay.at[i],
            dst_ref=vis.at[i, plane_of(EACH - 1)],
            send_sem=relay_sems.at[2, i],
            recv_sem=vis_sems.at[1, EACH * i + EACH - 1],
            device_id=at_band((VIA + 3 - BANDS) * way_on),
            device_id_type=MESH,
        )

    def begin_passing():
        if split_ways:
            for i in range(2):
                for n in (EACH * i, EACH * i + 1):
                    passing(n).start()
                first_leg(i).start()
            first_leg(2).start()
        else:
            for n in range(AHEAD):
                passing(n).start()

    def pass_on(n):
        if not split_ways:

            @pl.when(n + AHEAD < UNITS)
            def _():
                passing(n + AHEAD).start()

            return

        @pl.when((n % EACH != EACH - 1) & (n + 2 * EACH < UNITS))
        def _():
            passing(n + 2 * EACH).start()

        @pl.when(n == 0)
        def _():
            first_leg(0).wait_recv()
            second_leg(0).start()

        @pl.when((n % EACH == 1) & (n + EACH < UNITS))
        def _():
            first_leg(n // EACH + 1).wait_recv()
            second_leg(n // EACH + 1).start()

        @pl.when(n == 1)
        def _():
            first_leg(CHUNKS - 1).start()

    def end_passing():
        for n in range(UNITS):
            if split_ways and n % EACH == EACH - 1:
                first_leg(n // EACH).wait_send()
                second_leg(n // EACH).wait_send()
            else:
                passing(n).wait_send()

    def unit_row(unit, part, b):
        return unit * ROOM + part * 3 + b

    def densities(n):
        c, p = n // EACH, n % EACH
        visiting = repeated(vis, c, p)
        rep[c, p] = visiting
        value = right(own[p] * visiting, zh_ref[...], zl_ref[...])
        value = left(y_out_ref[...], value)
        spread(send1, c, p, value)

    def spread(send, c, unit, value):
        for part in range(EACH):
            for b in range(3):
                send[c, pl.ds(unit_row(unit, part, b), SIDE, stride=PITCH), :] = value[
                    part * SIDE : (part + 1) * SIDE, b * 128 : (b + 1) * 128
                ]

    def gathered(recv, c, row):
        return jnp.concatenate(
            [
                jnp.concatenate(
                    [recv[c, pl.ds(row(unit, b), SIDE, stride=PITCH), :] for b in range(3)], 1
                )
                for unit in range(EACH)
            ],
            0,
        )

    def rows_at(device, unit):
        return pl.ds(pl.multiple_of(device * PITCH + unit * ROOM, 8), ROWS)

    def exchange(way, n, send, recv):
        c, unit = n // EACH, n % EACH

        def one(t, _):
            to = (me + t) % SIDE
            pltpu.make_async_remote_copy(
                src_ref=send.at[c, rows_at(to, unit)],
                dst_ref=recv.at[c, rows_at(me, unit)],
                send_sem=send_sem.at[way, c],
                recv_sem=recv_sem.at[way, c],
                device_id={"grid": to},
                device_id_type=MESH,
            ).start()
            return 0

        lax.fori_loop(1, SIDE, one, 0)
        mine = rows_at(me, unit)
        pltpu.make_async_copy(send.at[c, mine], recv.at[c, mine], own_sem.at[way, c]).start()

    all_own = pl.ds(0, EACH * ROWS)
    all_others = pl.ds(0, (SIDE - 1) * EACH * ROWS)

    def arrived(way, c, recv):
        own_part, other_part = recv.at[c, all_own], recv.at[c, all_others]
        pltpu.make_async_copy(own_part, own_part, own_sem.at[way, c]).wait()
        pltpu.make_async_copy(other_part, other_part, recv_sem.at[way, c]).wait()

    def sent(way, c, send):
        part = send.at[c, all_others]
        pltpu.make_async_copy(part, part, send_sem.at[way, c]).wait()

    lane = lax.broadcasted_iota(jnp.int32, (1, LANES), 1)

    def weight_of(c):
        weights = [mask_ref[i, c].astype(jnp.float32) for i in range(4)]
        return jnp.where(
            lane < 2 * N,
            jnp.where(lane < N, weights[0], weights[1]),
            jnp.where(lane < 3 * N, weights[2], weights[3]),
        )

    def along_x(n):
        c, k = n // EACH, n % EACH
        weight = weight_of(c)
        value = gathered(recv1, c, lambda p, b: unit_row(p, k, b))
        spectrum = left(x_into_ref[...], value)
        value = spectrum * coulomb[k]
        for d in range(4):
            product = value * turned(spectrum, d)
            total = product[:8]
            for r in range(8, N, 8):
                total = total + product[r : r + 8]
            gram[d] += total * weight
        value = left(x_out_ref[...], value)
        spread(send2, c, k, value)

    def fields(n):
        c, p = n // EACH, n % EACH
        value = gathered(recv2, c, lambda k, b: unit_row(k, p, b))
        value = left(y_into_ref[...], value)
        value = right(value, zh_ref[...], zl_ref[...])
        field[p] = field[p] - value * rep[c, p] * weight_of(c)

    def prepare(p, _):
        own[p] = side_by_side(orb_ref, p)
        return 0

    for n in range(UNITS):
        loading(n).wait()
    pl.semaphore_wait(barrier, SIDE - 1 + len(sources))
    begin_passing()
    lax.fori_loop(0, EACH, prepare, 0)
    for load in table_loads:
        load.wait()
    gram[...] = jnp.zeros_like(gram)
    field[...] = jnp.zeros_like(field)
    coul = BOX * BOX / math.pi / (N * N * N)
    for k in range(EACH):
        ky = me * EACH + k
        folded = jnp.where(ky * 2 >= N, ky - N, ky).astype(jnp.float32)
        squares = sq_ref[...] + folded * folded
        coulomb[k] = jnp.where(squares > 0.5, coul / jnp.maximum(squares, 1.0), 0.0)

    def tell_sums():
        sums = [jnp.sum(gram[d], axis=0, keepdims=True) for d in range(4)]
        sums = jnp.concatenate(sums + [jnp.zeros((4, LANES), jnp.float32)], 0)
        high = sums.astype(jnp.bfloat16)
        middle, low = split(sums - high.astype(jnp.float32))
        pick = pick_ref[...]
        sums = dot(high, pick) + dot(middle, pick) + dot(low, pick)
        part_send[...] = sums
        part_recv[me] = sums

        def tell(t, _):
            pltpu.make_async_remote_copy(
                src_ref=part_send,
                dst_ref=part_recv.at[me],
                send_sem=part_sems.at[0],
                recv_sem=part_sems.at[1],
                device_id={"grid": (me + t) % SIDE},
                device_id_type=MESH,
            ).start()
            return 0

        lax.fori_loop(1, SIDE, tell, 0)

    def storing(p, i):
        return pltpu.make_async_copy(
            vis.at[i, pl.ds(pl.multiple_of(p * PLANE, 8), PLANE)],
            field_ref.at[p, :, i, :],
            load_sems.at[p * 4 + i],
        )

    def lay_out(p):
        tiles = [
            [field[p, 24 * u : 24 * u + 24, 128 * t : 128 * t + 128] for t in range(3)]
            for u in range(4)
        ]
        for i in range(4):
            rows = joined([taken(tiles[u], i) for u in range(4)])
            for t in range(3):
                vis[i, pl.ds(p * PLANE + t, 24, stride=3), :] = rows[t]
        for i in range(4):
            storing(p, i).start()

    def turn(n, _):
        @pl.when(n < UNITS)
        def _():
            passing(n).wait_recv()

            pass_on(n)
            densities(n)
            exchange(0, n, send1, recv1)

        m = n - X_AFTER

        @pl.when((m >= 0) & (m < UNITS))
        def _():
            @pl.when(m % EACH == 0)
            def _():
                arrived(0, m // EACH, recv1)

            along_x(m)
            exchange(1, m, send2, recv2)

        @pl.when(m == UNITS - 1)
        def _():
            tell_sums()

        f = n - Y_AFTER

        @pl.when(f >= 0)
        def _():
            @pl.when(f % EACH == 0)
            def _():
                arrived(1, f // EACH, recv2)

            fields(f)

        @pl.when(f >= UNITS - EACH)
        def _():
            lay_out(f % EACH)

        return 0

    lax.fori_loop(0, UNITS + Y_AFTER, turn, 0)

    end_passing()
    for c in range(CHUNKS):
        sent(0, c, send1)
        sent(1, c, send2)
    others = part_recv.at[pl.ds(0, SIDE - 1)]
    pltpu.make_async_copy(others, others, part_sems.at[1]).wait()
    pltpu.make_async_copy(others, others, part_sems.at[0]).wait()
    sums = jnp.sum(part_recv[...], axis=0) * (-1.0 / (N * N * N))
    apart = lax.broadcasted_iota(jnp.int32, (8, 128), 0) - lax.broadcasted_iota(jnp.int32, (8, 128), 1)
    result = jnp.zeros((8, 128), jnp.float32)
    for d in range(4):
        result = jnp.where((apart + 128) % 4 == d, sums[d : d + 1], result)
    proj_ref[...] = result[:4, :4]
    for n in range(UNITS):
        storing(n // 4, n % 4).wait()


def vmem(count):
    return [pl.BlockSpec(memory_space=pltpu.VMEM)] * count


def at_distance(distance, mask, orbitals, *constants):
    def scratch(*shape):
        return pltpu.VMEM(shape, jnp.float32)

    buffer = scratch(CHUNKS, SIDE * PITCH, 128)
    return pl.pallas_call(
        functools.partial(body, distance),
        out_shape=(
            jax.ShapeDtypeStruct((EACH, PLANE, 4, 128), jnp.float32),
            jax.ShapeDtypeStruct((4, 4), jnp.float32),
        ),
        in_specs=[pl.BlockSpec(memory_space=pltpu.SMEM)]
        + [pl.BlockSpec(memory_space=pltpu.HBM)] * (1 + len(constants)),
        out_specs=tuple(vmem(2)),
        scratch_shapes=[
            scratch(4, FLAT, 128),
            *[pltpu.VMEM(table.shape, table.dtype) for table in constants],
            scratch(4, FLAT, 128),
            scratch(4, PLANE, 128),
            scratch(EACH, N, LANES),
            scratch(4, 8, LANES),
            scratch(4, EACH, N, LANES),
            scratch(EACH, N, LANES),
            scratch(EACH, N, LANES),
            buffer, buffer, buffer, buffer,
            scratch(8, 128),
            scratch(SIDE, 8, 128),
            pltpu.SemaphoreType.DMA((2, UNITS)),
            pltpu.SemaphoreType.DMA((3, 4)),
            pltpu.SemaphoreType.DMA((2, CHUNKS)),
            pltpu.SemaphoreType.DMA((2, CHUNKS)),
            pltpu.SemaphoreType.DMA((2, CHUNKS)),
            pltpu.SemaphoreType.DMA((2,)),
            pltpu.SemaphoreType.DMA((UNITS + 8,)),
        ],
        compiler_params=pltpu.CompilerParams(
            collective_id=distance - 1, has_side_effects=True, vmem_limit_bytes=40 * 1024 * 1024
        ),
        name=f"exchange_{distance}",
    )(mask, orbitals, *constants)


def shards(orbitals, pair_mask, cycle_step):
    constants = [jnp.asarray(t) for t in tables()]
    field, projection = lax.switch(
        cycle_step - 1,
        [functools.partial(at_distance, d) for d in range(1, BANDS)],
        pair_mask,
        orbitals.reshape(4, EACH, PLANE, 128).transpose(1, 2, 0, 3),
        *constants,
    )
    return field.transpose(2, 0, 1, 3).reshape(4, EACH, N * N), projection


def solution(mesh):
    return jax.shard_map(
        shards,
        mesh=mesh,
        in_specs=(P("band", "grid", None), P("band", None), P()),
        out_specs=(P("band", "grid", None), P("band", None)),
        check_vma=False,
    )
```
